512 devices in a mesh: dp: 4 (over x), ctx: 16 (over y, core), tensor: 8 (over z).
Axes of the slice: x: 4, y: 8, z: 8, core: 2. Of those that a mesh axis runs over, the one named last changes fastest.
Arguments:
- tokens: bfloat16 [8192, 8192], P(('dp', 'tensor'), 'ctx'), parts along dimension 0, may hold values from -6 to 6
- queries: bfloat16 [8192, 8192], P(('dp', 'ctx'), 'tensor'), parts along dimension 0, may hold values from -100 to 100
- key_value_weight: bfloat16 [8192, 2048], P('ctx', 'tensor'), may hold values from -0.0625 to 0.0625
- out_weight: bfloat16 [8192, 8192], P('tensor', 'ctx'), may hold values from -0.0625 to 0.0625
- doc_lengths: int32 [32], P('dp'), parts along dimension 0, may hold values from 1 to 1024, 2048 in all
- block_order: int32 [128], P('dp'), parts along dimension 0, may hold values from 0 to 31, each once
Outputs:
- mixed: bfloat16 [8192, 8192], P(('dp', 'tensor'), 'ctx'), parts along dimension 0
The draws below stay inside these ranges and needn't reach their ends.
There are 4 independent parts, one for each index of `dp`. The reference program is written for one: setup_inputs(seed, part) draws one part's arguments, and reference() takes and returns one part's arrays. A program takes and returns all parts, laid end to end along the dimension named above; an argument that names none is the same for every part. Nothing has to cross between parts.
Inputs may be any that keep to these rules, and one draw needn't show every extreme that they name: `doc_lengths`: the lengths add up to 2048. `block_order`: each of 0 to 31 once.
All inputs are finite; a program needn't handle non-finite values.
Results may differ from the reference program's by a relative error of at most 0.014.
Values may be sent and summed in bfloat16 or wider, within the bound.
No kernel may reach another device: no remote copies, remote signals or barrier semaphores. Data moves between devices by JAX's collectives and lax.ppermute only.
A program may use at most 64 MiB of HBM per device.

```python
import math
import jax
import jax.numpy as jnp
import numpy as np
from jax import lax

MODEL_WIDTH = 8192
QUERY_HEADS = 64
KEY_VALUE_HEADS = 8
HEAD_WIDTH = 128
T_DEV = 128
NDOCS = 8
SEQUENCE_TOKENS = 2048
HEAD_GROUPS = 8
N_CTX = 16


def draw_queries(key, part):
    first, second = jax.random.split(jax.random.fold_in(key, 7), 2)
    base = 0.7 * jnp.clip(jax.random.normal(first, (SEQUENCE_TOKENS, QUERY_HEADS * HEAD_WIDTH), jnp.float32), -4.0, 4.0)
    spread = jnp.exp(jax.random.uniform(second, (SEQUENCE_TOKENS, 1), jnp.float32, jnp.log(0.5), jnp.log(2.0)))
    return (base * spread).astype(jnp.bfloat16)


def level_of(key, shape, shards, smallest, largest):
    gain, own = 1.0, jax.random.fold_in(key, 6)
    for dim, parts in shards:
        steps = jnp.exp(jax.random.uniform(jax.random.fold_in(own, dim), (parts,), jnp.float32, smallest / len(shards), largest / len(shards)))
        gain = gain * jnp.repeat(steps, shape[dim] // parts).reshape([-1 if axis == dim else 1 for axis in range(len(shape))])
    return gain


def split_up(number_of, total, bound, slope):
    portions = [(1 << 20) // math.isqrt(grade ** slope) + 1 for grade in range(2, number_of + 1)]
    rest, given = total - bound - (number_of - 1), [1] * (number_of - 1)
    while rest > 0:
        candidates = [i for i in range(number_of - 1) if given[i] < bound]
        pool, budget = sum([portions[i] for i in candidates]), rest
        for i in candidates:
            more = min(bound - given[i], max(1, budget * portions[i] // pool), rest)
            given[i] = given[i] + more
            rest = rest - more
    return np.array([bound] + given)


def uneven(own_key, count, total, most, lean):
    if count == 2:
        one = jax.random.randint(own_key, (), max(1, total - most), min(most, total - 1) + 1)
        return jnp.stack([one, total - one])
    sizes = jnp.asarray(split_up(count, total, most, lean), jnp.int32)
    couples = (count - 1) // 2
    source_of, receiver = sizes[1:1 + 2 * couples:2], sizes[2:2 + 2 * couples:2]
    room = jnp.minimum(source_of - 1, most - receiver)
    passed = jax.random.randint(jax.random.fold_in(own_key, 1), (couples,), 0, 1 << 20) % (room + 1)
    sizes = sizes.at[1:1 + 2 * couples:2].set(source_of - passed).at[2:2 + 2 * couples:2].set(receiver + passed)
    return sizes[jax.random.permutation(jax.random.fold_in(own_key, 2), count)]


def centred(key, dims, scale, bound, shards=(), kind=jnp.bfloat16):
    gain = level_of(key, dims, shards, -0.22, 0.18) if shards else 1.0
    array = jax.random.normal(key, dims, jnp.float32) * scale * gain
    return jnp.minimum(jnp.maximum(array, -bound), bound).astype(kind)


def setup_inputs(seed: int = 0, part: int = 0) -> dict:
    arg_keys = jax.random.split(jax.random.key(seed), 7)
    part_keys = jax.random.split(jax.random.fold_in(arg_keys[6], part), 7)
    return {
        "tokens": centred(part_keys[0], (SEQUENCE_TOKENS, MODEL_WIDTH), 1.0, 6.0, ((0, 8), (1, 16))),
        "queries": draw_queries(jax.random.fold_in(jax.random.fold_in(arg_keys[6], part), 71), part),
        "key_value_weight": centred(arg_keys[2], (MODEL_WIDTH, 2 * KEY_VALUE_HEADS * HEAD_WIDTH), MODEL_WIDTH ** -0.5, 0.0625, ((0, 16), (1, 8))),
        "out_weight": centred(arg_keys[3], (QUERY_HEADS * HEAD_WIDTH, MODEL_WIDTH), (QUERY_HEADS * HEAD_WIDTH) ** -0.5, 0.0625, ((0, 8), (1, 16))),
        "doc_lengths": uneven(part_keys[4], NDOCS, SEQUENCE_TOKENS, SEQUENCE_TOKENS // 2, 2).astype(jnp.int32),
        "block_order": jax.random.permutation(part_keys[5], 2 * N_CTX).astype(jnp.int32),
    }


def doc_index(positions, doc_ends):
    return lax.optimization_barrier(jnp.sum((doc_ends[None, :] <= positions[:, None]).astype(jnp.int32), axis=1)).astype(jnp.int32)

def reference(tokens, queries, key_value_weight, out_weight, doc_lengths, block_order):
    key_value_full = jnp.dot(tokens, key_value_weight, preferred_element_type=jnp.float32).astype(jnp.bfloat16)
    key_value_full = key_value_full.reshape(SEQUENCE_TOKENS, KEY_VALUE_HEADS, 2, HEAD_WIDTH)
    half_rows = T_DEV // 2
    query_pos = (jnp.repeat(block_order.astype(jnp.int32), half_rows) * half_rows + jnp.tile(jnp.arange(half_rows, dtype=jnp.int32), 2 * N_CTX)).astype(jnp.int32)
    key_pos = jnp.arange(SEQUENCE_TOKENS, dtype=jnp.int32)
    doc_ends = jnp.cumsum(doc_lengths).astype(jnp.int32)
    query_doc = doc_index(query_pos, doc_ends)
    key_doc = doc_index(key_pos, doc_ends)
    allowed = (query_doc[:, None] == key_doc[None, :]) & (key_pos[None, :] <= query_pos[:, None])
    queries_per_group = QUERY_HEADS // KEY_VALUE_HEADS
    query_groups = jnp.transpose(queries.reshape(SEQUENCE_TOKENS, KEY_VALUE_HEADS, queries_per_group, HEAD_WIDTH), (1, 0, 2, 3))
    keys_all = jnp.transpose(key_value_full[:, :, 0, :], (1, 0, 2))
    values_all = jnp.transpose(key_value_full[:, :, 1, :], (1, 0, 2))
    scale = 1.0 / jnp.sqrt(jnp.float32(HEAD_WIDTH))

    def one_group(operands):
        query_head, key_head, value_head = operands
        scores = jnp.einsum('tgd,nd->tgn', query_head.astype(jnp.float32), key_head.astype(jnp.float32)) * scale
        masked = jnp.where(allowed[:, None, :], scores, jnp.float32(-1e+30))
        top_score = lax.optimization_barrier(jnp.max(masked, axis=-1))
        probs = jnp.where(allowed[:, None, :], jnp.exp(scores - top_score[..., None]), jnp.float32(0.0))
        total = lax.optimization_barrier(jnp.sum(probs, axis=-1))
        weighted = jnp.einsum('tgn,nd->tgd', probs.astype(jnp.bfloat16).astype(jnp.float32), value_head.astype(jnp.float32))
        return weighted / total[..., None]
    heads_out = lax.map(one_group, (query_groups, keys_all, values_all))
    attn = jnp.transpose(heads_out, (1, 0, 2, 3)).reshape(SEQUENCE_TOKENS, QUERY_HEADS * HEAD_WIDTH).astype(jnp.bfloat16)
    group_width = QUERY_HEADS * HEAD_WIDTH // HEAD_GROUPS
    mixed = jnp.zeros((SEQUENCE_TOKENS, MODEL_WIDTH), jnp.float32)
    for group in range(HEAD_GROUPS):
        part_out = jnp.dot(attn[:, group * group_width:(group + 1) * group_width], out_weight[group * group_width:(group + 1) * group_width, :], preferred_element_type=jnp.float32).astype(jnp.bfloat16)
        part_out = lax.optimization_barrier(part_out)
        mixed = mixed + part_out.astype(jnp.float32)
    return mixed.astype(jnp.bfloat16)
```

```python
import functools
import math

import jax
import jax.numpy as jnp
from jax import lax
from jax.experimental import pallas as pl
from jax.experimental.pallas import tpu as pltpu
from jax.sharding import Mesh, PartitionSpec as P

HEAD = 128
RING = 8
BLOCK = 64
KEYS = 256
NEG = -1e30
EXP_SCALE = math.log2(math.e) / math.sqrt(HEAD)


def attend_kernel(base, gap, ids, lengths, order, q_ref, kv_ref, out_ref, acc_ref, top_ref):
    step = pl.program_id(0)
    unit = step // 2
    z, core = ids[0], ids[2]
    owner = (z + base + unit + gap * (unit // 2)) % RING
    first = order[(owner * 2 + core) * 2 + step % 2] * BLOCK
    heads = q_ref.shape[1] // HEAD
    rows = BLOCK * heads

    row_pos = first + lax.broadcasted_iota(jnp.int32, (BLOCK, KEYS), 0)
    row_start = jnp.zeros((BLOCK, KEYS), jnp.int32)
    lowest = jnp.int32(0)
    end = jnp.int32(0)
    for j in range(lengths.shape[0]):
        end = end + lengths[j]
        row_start = jnp.where(row_pos >= end, end, row_start)
        lowest = jnp.where(first >= end, end, lowest)
    columns = lax.broadcasted_iota(jnp.int32, (BLOCK, KEYS), 1)

    query = jnp.concatenate(
        [q_ref[:, h * HEAD : (h + 1) * HEAD] for h in range(heads)], axis=0
    )
    ones = jnp.ones((KEYS, HEAD), jnp.bfloat16)
    acc_ref[...] = jnp.zeros_like(acc_ref)
    top_ref[...] = jnp.full_like(top_ref, NEG)
    last = first // KEYS

    @pl.loop(0, last - lowest // KEYS + 1)
    def _(i):
        block = last - i
        offset = pl.multiple_of(((block - z + RING) % RING) * KEYS, KEYS)
        keys = kv_ref[pl.ds(offset, KEYS), :HEAD]
        values = kv_ref[pl.ds(offset, KEYS), HEAD:]
        scores = lax.dot_general(
            query, keys, (((1,), (1,)), ((), ())), preferred_element_type=jnp.float32
        )
        key_pos = block * KEYS + columns
        allowed = (key_pos >= row_start) & (key_pos <= row_pos)
        scores = jnp.where(
            allowed[None], scores.reshape(heads, BLOCK, KEYS), jnp.float32(NEG)
        ).reshape(rows, KEYS)
        old = top_ref[...]
        new = jnp.maximum(old, jnp.max(scores, axis=1, keepdims=True))
        top_ref[...] = new
        keep = jnp.exp2((old - new) * EXP_SCALE)
        probs = jnp.exp2((scores - new[:, :1]) * EXP_SCALE).astype(jnp.bfloat16)
        both = jnp.concatenate([values, ones], axis=1)
        acc_ref[...] = acc_ref[...] * keep[:, :1] + jnp.dot(
            probs, both, preferred_element_type=jnp.float32
        )

    for h in range(heads):
        part = acc_ref[h * BLOCK : (h + 1) * BLOCK, :]
        out_ref[:, h * HEAD : (h + 1) * HEAD] = (part[:, :HEAD] / part[:, HEAD:]).astype(
            out_ref.dtype
        )


def attend(base, gap, units, ids, lengths, order, queries, kv):
    width = queries.shape[1]
    heads = width // HEAD

    def q_map(i, ids, lengths, order):
        unit = i // 2
        block = (ids[0] + base + unit + gap * (unit // 2) - ids[1] + RING) % RING
        return (block * 2 + i % 2, 0)

    return pl.pallas_call(
        functools.partial(attend_kernel, base, gap),
        out_shape=jax.ShapeDtypeStruct((units * 2 * BLOCK, width), jnp.bfloat16),
        grid_spec=pltpu.PrefetchScalarGridSpec(
            num_scalar_prefetch=3,
            grid=(units * 2,),
            in_specs=[
                pl.BlockSpec((BLOCK, width), q_map),
                pl.BlockSpec(kv.shape, lambda i, *_: (0, 0)),
            ],
            out_specs=pl.BlockSpec((BLOCK, width), lambda i, *_: (i, 0)),
            scratch_shapes=[
                pltpu.VMEM((BLOCK * heads, 2 * HEAD), jnp.float32),
                pltpu.VMEM((BLOCK * heads, HEAD), jnp.float32),
            ],
        ),
        cost_estimate=pl.CostEstimate(
            flops=units * 600_000_000, bytes_accessed=units * 1_000_000, transcendentals=units * 500_000
        ),
        name="attend",
    )(ids, lengths, order, queries, kv)


def shift(x, axis, by):
    return lax.ppermute(x, axis, [(i, (i + by) % RING) for i in range(RING)])


def swap(x):
    return lax.ppermute(x, "core", [(0, 1), (1, 0)])


def gather_rounds(x, axis):
    half = x.shape[0] // 2
    up, down = shift(x, axis, -1), shift(x, axis, 1)
    yield (up, down)
    up2 = shift(jnp.concatenate([x, up], axis=0), axis, -2)
    down2 = shift(jnp.concatenate([down, x], axis=0), axis, 2)
    yield (up2, down2)
    rows = x.shape[0]
    far_top = shift(down2[:half], axis, 1)
    far_bottom = shift(up2[rows + half :], axis, -1)
    yield (far_top, far_bottom)


def local(tokens, queries, key_value_weight, out_weight, doc_lengths, block_order):
    z, y, core = lax.axis_index("z"), lax.axis_index("y"), lax.axis_index("core")
    ids = jnp.stack([z, y, core]).astype(jnp.int32)
    other_weight = swap(out_weight)

    def project(block):
        return jnp.dot(block, key_value_weight, preferred_element_type=jnp.float32)

    token_rounds, query_rounds = gather_rounds(tokens, "z"), gather_rounds(queries, "y")
    (t_up, t_down), (q_up, q_down) = next(token_rounds), next(query_rounds)
    (t_up2, t_down2), (q_up2, q_down2) = next(token_rounds), next(query_rounds)
    t_far, q_far = next(token_rounds), next(query_rounds)
    partial_kv = jnp.concatenate(
        [project(b) for b in (tokens, t_up, t_up2, *t_far, t_down2, t_down)], axis=0
    )
    all_queries = jnp.concatenate([queries, q_up, q_up2, *q_far, q_down2, q_down], axis=0)
    partial_kv, all_queries, other_weight = lax.optimization_barrier(
        (partial_kv, all_queries, other_weight)
    )
    kv = lax.psum(partial_kv, ("y", "core")).astype(jnp.bfloat16)

    def products(base, gap, units):
        attn = attend(base, gap, units, ids, doc_lengths, block_order, all_queries, kv)
        return tuple(
            jnp.dot(attn, w, preferred_element_type=jnp.float32) for w in (out_weight, other_weight)
        )

    rows = queries.shape[0]
    f32, bf16 = jnp.float32, jnp.bfloat16

    def both(parts, unit):
        return jnp.concatenate([p[unit * rows : (unit + 1) * rows] for p in parts], axis=1)

    far = products(4, 0, 1)
    far_up, far_down = shift(far[0].astype(bf16), "z", 1), shift(far[1].astype(bf16), "z", -1)
    middle = products(2, 1, 4)
    width = far_up.shape[1]
    zero = jnp.zeros((rows, width), f32)
    third = both(middle, 1) + jnp.concatenate([far_up.astype(f32), zero], axis=1)
    minus_third = both(middle, 2) + jnp.concatenate([zero, far_down.astype(f32)], axis=1)
    up2 = shift(jnp.concatenate([both(middle, 0), third], axis=0).astype(bf16), "z", 2)
    down2 = shift(jnp.concatenate([both(middle, 3), minus_third], axis=0).astype(bf16), "z", -2)
    near = products(7, 0, 3)
    up1 = shift((both(near, 2) + up2[rows:].astype(f32)).astype(bf16), "z", 1)
    down1 = shift((both(near, 0) + down2[rows:].astype(f32)).astype(bf16), "z", -1)
    total = (
        both(near, 1)
        + up2[:rows].astype(f32)
        + down2[:rows].astype(f32)
        + up1.astype(f32)
        + down1.astype(f32)
    ).astype(bf16)
    mine, theirs = total[:, :width], swap(total[:, width:])
    return jnp.where(
        core == 0,
        jnp.concatenate([mine, theirs], axis=0),
        jnp.concatenate([theirs, mine], axis=0),
    )


def solution(mesh):
    fine = Mesh(mesh.devices.reshape(4, 8, 2, 8), ("dp", "y", "core", "z"))
    ctx = ("y", "core")
    in_specs = (
        P(("dp", "z"), ctx),
        P(("dp", "y", "core"), "z"),
        P(ctx, "z"),
        P("z", ctx),
        P("dp"),
        P("dp"),
    )
    return jax.shard_map(
        local, mesh=fine, in_specs=in_specs, out_specs=P(("dp", "z"), ctx), check_vma=False
    )
```

```python
import functools
import math

import jax
import jax.numpy as jnp
from jax import lax
from jax.experimental import pallas as pl
from jax.experimental.pallas import tpu as pltpu
from jax.sharding import Mesh, PartitionSpec as P


HEAD = 128
RING = 8
BLOCK = 64
KEYS = 256
NEG = -1e30
EXP_SCALE = math.log2(math.e) / math.sqrt(HEAD)


def attend_kernel(base, gap, ids, lengths, order, q_ref, kv_ref, out_ref, acc_ref, top_ref):
    step = pl.program_id(0)
    unit = step // 2
    z, core = ids[0], ids[2]
    owner = (z + base + unit + gap * (unit // 2)) % RING
    first = order[(owner * 2 + core) * 2 + step % 2] * BLOCK
    heads = q_ref.shape[1] // HEAD
    rows = BLOCK * heads

    row_pos = first + lax.broadcasted_iota(jnp.int32, (BLOCK, KEYS), 0)
    row_start = jnp.zeros((BLOCK, KEYS), jnp.int32)
    lowest = jnp.int32(0)
    end = jnp.int32(0)
    for j in range(lengths.shape[0]):
        end = end + lengths[j]
        row_start = jnp.where(row_pos >= end, end, row_start)
        lowest = jnp.where(first >= end, end, lowest)
    columns = lax.broadcasted_iota(jnp.int32, (BLOCK, KEYS), 1)

    query = jnp.concatenate(
        [q_ref[:, h * HEAD : (h + 1) * HEAD] for h in range(heads)], axis=0
    )
    ones = jnp.ones((KEYS, HEAD), jnp.bfloat16)
    acc_ref[...] = jnp.zeros_like(acc_ref)
    top_ref[...] = jnp.full_like(top_ref, NEG)
    last = first // KEYS

    @pl.loop(0, last - lowest // KEYS + 1)
    def _(i):
        block = last - i
        offset = pl.multiple_of(((block - z + RING) % RING) * KEYS, KEYS)
        keys = kv_ref[pl.ds(offset, KEYS), :HEAD]
        values = kv_ref[pl.ds(offset, KEYS), HEAD:]
        scores = lax.dot_general(
            query, keys, (((1,), (1,)), ((), ())), preferred_element_type=jnp.float32
        )
        key_pos = block * KEYS + columns
        allowed = (key_pos >= row_start) & (key_pos <= row_pos)
        scores = jnp.where(
            allowed[None], scores.reshape(heads, BLOCK, KEYS), jnp.float32(NEG)
        ).reshape(rows, KEYS)
        old = top_ref[...]
        new = jnp.maximum(old, jnp.max(scores, axis=1, keepdims=True))
        top_ref[...] = new
        keep = jnp.exp2((old - new) * EXP_SCALE)
        wide = jnp.concatenate([new, new], axis=1)
        probs = jnp.exp2((scores - wide) * EXP_SCALE).astype(jnp.bfloat16)
        both = jnp.concatenate([values, ones], axis=1)
        acc_ref[...] = acc_ref[...] * jnp.concatenate([keep, keep], axis=1) + jnp.dot(
            probs, both, preferred_element_type=jnp.float32
        )

    for h in range(heads):
        part = acc_ref[h * BLOCK : (h + 1) * BLOCK, :]
        out_ref[:, h * HEAD : (h + 1) * HEAD] = (part[:, :HEAD] / part[:, HEAD:]).astype(
            out_ref.dtype
        )


def attend(base, gap, units, ids, lengths, order, queries, kv):
    width = queries.shape[1]
    heads = width // HEAD

    def q_map(i, ids, lengths, order):
        unit = i // 2
        block = (ids[0] + base + unit + gap * (unit // 2) - ids[1] + RING) % RING
        return (block * 2 + i % 2, 0)

    return pl.pallas_call(
        functools.partial(attend_kernel, base, gap),
        out_shape=jax.ShapeDtypeStruct((units * 2 * BLOCK, width), jnp.bfloat16),
        grid_spec=pltpu.PrefetchScalarGridSpec(
            num_scalar_prefetch=3,
            grid=(units * 2,),
            in_specs=[
                pl.BlockSpec((BLOCK, width), q_map),
                pl.BlockSpec(kv.shape, lambda i, *_: (0, 0)),
            ],
            out_specs=pl.BlockSpec((BLOCK, width), lambda i, *_: (i, 0)),
            scratch_shapes=[
                pltpu.VMEM((BLOCK * heads, 2 * HEAD), jnp.float32),
                pltpu.VMEM((BLOCK * heads, HEAD), jnp.float32),
            ],
        ),
        cost_estimate=pl.CostEstimate(
            flops=units * 600_000_000, bytes_accessed=units * 1_000_000, transcendentals=units * 500_000
        ),
        name="attend",
    )(ids, lengths, order, queries, kv)


def shift(x, axis, by):
    return lax.ppermute(x, axis, [(i, (i + by) % RING) for i in range(RING)])


def swap(x):
    return lax.ppermute(x, "core", [(0, 1), (1, 0)])


def local(tokens, queries, key_value_weight, out_weight, doc_lengths, block_order):
    z, y, core = lax.axis_index("z"), lax.axis_index("y"), lax.axis_index("core")
    ids = jnp.stack([z, y, core]).astype(jnp.int32)
    other_weight = swap(out_weight)

    def project(block):
        return jnp.dot(block, key_value_weight, preferred_element_type=jnp.float32)

    size = tokens.shape[0]
    t_up, t_down = shift(tokens, "z", -1), shift(tokens, "z", 1)
    t_up2 = shift(jnp.concatenate([tokens, t_up], axis=0), "z", -2)
    t_down2 = shift(jnp.concatenate([t_down, tokens], axis=0), "z", 2)
    t_top = shift(t_down2[: size // 2], "z", 1)
    t_bottom = shift(t_up2[size + size // 2 :], "z", -1)

    q_far = shift(queries, "y", 4)
    q_up, q_down = shift(queries, "y", -1), shift(queries, "y", 1)
    q_up2 = shift(jnp.concatenate([queries, q_up], axis=0), "y", -2)
    q_down2 = shift(jnp.concatenate([q_down, queries], axis=0), "y", 2)

    partial_kv = jnp.concatenate(
        [project(b) for b in (tokens, t_up, t_up2, t_top, t_bottom, t_down2, t_down)], axis=0
    )
    kv = lax.psum(partial_kv, ("y", "core"))
    kv = kv.astype(jnp.bfloat16)
    all_queries = jnp.concatenate([queries, q_up, q_up2, q_far, q_down2, q_down], axis=0)

    def products(base, gap, units):
        attn = attend(base, gap, units, ids, doc_lengths, block_order, all_queries, kv)
        return tuple(
            jnp.dot(attn, w, preferred_element_type=jnp.float32) for w in (out_weight, other_weight)
        )

    rows = queries.shape[0]
    f32, bf16 = jnp.float32, jnp.bfloat16

    def both(parts, unit):
        return jnp.concatenate([p[unit * rows : (unit + 1) * rows] for p in parts], axis=1)

    far = products(4, 0, 1)
    far_up = shift(far[0].astype(bf16), "z", 1)
    far_down = shift(far[1].astype(bf16), "z", -1)
    middle = products(2, 1, 4)
    width = far_up.shape[1]
    zero = jnp.zeros((rows, width), f32)
    third = both(middle, 1) + jnp.concatenate([far_up.astype(f32), zero], axis=1)
    minus_third = both(middle, 2) + jnp.concatenate([zero, far_down.astype(f32)], axis=1)
    up2 = shift(jnp.concatenate([both(middle, 0), third], axis=0).astype(bf16), "z", 2)
    down2 = shift(jnp.concatenate([both(middle, 3), minus_third], axis=0).astype(bf16), "z", -2)
    near = products(7, 0, 3)
    up1 = shift((both(near, 2) + up2[rows:].astype(f32)).astype(bf16), "z", 1)
    down1 = shift((both(near, 0) + down2[rows:].astype(f32)).astype(bf16), "z", -1)
    total = (
        both(near, 1)
        + up2[:rows].astype(f32)
        + down2[:rows].astype(f32)
        + up1.astype(f32)
        + down1.astype(f32)
    ).astype(bf16)
    mine, theirs = total[:, :width], swap(total[:, width:])
    return jnp.where(
        core == 0,
        jnp.concatenate([mine, theirs], axis=0),
        jnp.concatenate([theirs, mine], axis=0),
    )


def solution(mesh):
    fine = Mesh(mesh.devices.reshape(4, 8, 2, 8), ("dp", "y", "core", "z"))
    ctx = ("y", "core")
    in_specs = (
        P(("dp", "z"), ctx),
        P(("dp", "y", "core"), "z"),
        P(ctx, "z"),
        P("z", ctx),
        P("dp"),
        P("dp"),
    )
    return jax.shard_map(
        local, mesh=fine, in_specs=in_specs, out_specs=P(("dp", "z"), ctx), check_vma=False
    )
```

```python
import functools
import math

import jax
import jax.numpy as jnp
from jax import lax
from jax.experimental import pallas as pl
from jax.experimental.pallas import tpu as pltpu
from jax.sharding import Mesh, PartitionSpec as P


HEAD = 128
RING = 8
BLOCK = 64
KEYS = 256
NEG = -1e30
EXP_SCALE = math.log2(math.e) / math.sqrt(HEAD)


def attend_kernel(base, gap, ids, lengths, order, q_ref, kv_ref, out_ref, acc_ref, top_ref):
    step = pl.program_id(0)
    unit = step // 2
    z, core = ids[0], ids[1]
    owner = (z + base + unit + gap * (unit // 2)) % RING
    first = order[(owner * 2 + core) * 2 + step % 2] * BLOCK
    heads = q_ref.shape[1] // HEAD
    rows = BLOCK * heads

    row_pos = first + lax.broadcasted_iota(jnp.int32, (BLOCK, KEYS), 0)
    row_start = jnp.zeros((BLOCK, KEYS), jnp.int32)
    lowest = jnp.int32(0)
    end = jnp.int32(0)
    for j in range(lengths.shape[0]):
        end = end + lengths[j]
        row_start = jnp.where(row_pos >= end, end, row_start)
        lowest = jnp.where(first >= end, end, lowest)
    columns = lax.broadcasted_iota(jnp.int32, (BLOCK, KEYS), 1)

    query = jnp.concatenate(
        [q_ref[:, h * HEAD : (h + 1) * HEAD] for h in range(heads)], axis=0
    )
    ones = jnp.ones((KEYS, HEAD), jnp.bfloat16)
    acc_ref[...] = jnp.zeros_like(acc_ref)
    top_ref[...] = jnp.full_like(top_ref, NEG)
    last = first // KEYS

    @pl.loop(0, last - lowest // KEYS + 1)
    def _(i):
        block = last - i
        offset = pl.multiple_of(((block - z + RING) % RING) * KEYS, KEYS)
        keys = kv_ref[pl.ds(offset, KEYS), :HEAD]
        values = kv_ref[pl.ds(offset, KEYS), HEAD:]
        scores = lax.dot_general(
            query, keys, (((1,), (1,)), ((), ())), preferred_element_type=jnp.float32
        )
        key_pos = block * KEYS + columns
        allowed = (key_pos >= row_start) & (key_pos <= row_pos)
        scores = jnp.where(
            allowed[None], scores.reshape(heads, BLOCK, KEYS), jnp.float32(NEG)
        ).reshape(rows, KEYS)
        old = top_ref[...]
        new = jnp.maximum(old, jnp.max(scores, axis=1, keepdims=True))
        top_ref[...] = new
        keep = jnp.exp2((old - new) * EXP_SCALE)
        wide = jnp.concatenate([new, new], axis=1)
        probs = jnp.exp2((scores - wide) * EXP_SCALE).astype(jnp.bfloat16)
        both = jnp.concatenate([values, ones], axis=1)
        acc_ref[...] = acc_ref[...] * jnp.concatenate([keep, keep], axis=1) + jnp.dot(
            probs, both, preferred_element_type=jnp.float32
        )

    for h in range(heads):
        part = acc_ref[h * BLOCK : (h + 1) * BLOCK, :]
        out_ref[:, h * HEAD : (h + 1) * HEAD] = (part[:, :HEAD] / part[:, HEAD:]).astype(
            out_ref.dtype
        )


def attend(base, gap, units, ids, lengths, order, queries, kv):
    width = queries.shape[1]
    heads = width // HEAD

    def q_map(i, ids, lengths, order):
        unit = i // 2
        block = (ids[0] + base + unit + gap * (unit // 2)) % RING
        return (block * 2 + i % 2, 0)

    return pl.pallas_call(
        functools.partial(attend_kernel, base, gap),
        out_shape=jax.ShapeDtypeStruct((units * 2 * BLOCK, width), jnp.bfloat16),
        grid_spec=pltpu.PrefetchScalarGridSpec(
            num_scalar_prefetch=3,
            grid=(units * 2,),
            in_specs=[
                pl.BlockSpec((BLOCK, width), q_map),
                pl.BlockSpec(kv.shape, lambda i, *_: (0, 0)),
            ],
            out_specs=pl.BlockSpec((BLOCK, width), lambda i, *_: (i, 0)),
            scratch_shapes=[
                pltpu.VMEM((BLOCK * heads, 2 * HEAD), jnp.float32),
                pltpu.VMEM((BLOCK * heads, HEAD), jnp.float32),
            ],
        ),
        cost_estimate=pl.CostEstimate(
            flops=units * 600_000_000, bytes_accessed=units * 1_000_000, transcendentals=units * 500_000
        ),
        name="attend",
    )(ids, lengths, order, queries, kv)


def shift(x, axis, by):
    return lax.ppermute(x, axis, [(i, (i + by) % RING) for i in range(RING)])


def swap(x):
    return lax.ppermute(x, "core", [(0, 1), (1, 0)])


def local(tokens, queries, key_value_weight, out_weight, doc_lengths, block_order):
    z, core = lax.axis_index("z"), lax.axis_index("core")
    ids = jnp.stack([z, core]).astype(jnp.int32)
    other_weight = swap(out_weight)

    def project(block):
        return jnp.dot(block, key_value_weight, preferred_element_type=jnp.float32)

    size = tokens.shape[0]
    t_up, t_down = shift(tokens, "z", -1), shift(tokens, "z", 1)
    t_up2 = shift(jnp.concatenate([tokens, t_up], axis=0), "z", -2)
    t_down2 = shift(jnp.concatenate([t_down, tokens], axis=0), "z", 2)
    t_top = shift(t_down2[: size // 2], "z", 1)
    t_bottom = shift(t_up2[size + size // 2 :], "z", -1)

    all_queries = lax.all_gather(queries, "y", axis=0, tiled=True)

    partial_kv = jnp.concatenate(
        [project(b) for b in (tokens, t_up, t_up2, t_top, t_bottom, t_down2, t_down)], axis=0
    )
    kv = lax.psum(partial_kv, ("y", "core"))
    kv = kv.astype(jnp.bfloat16)

    def products(base, gap, units):
        attn = attend(base, gap, units, ids, doc_lengths, block_order, all_queries, kv)
        return tuple(
            jnp.dot(attn, w, preferred_element_type=jnp.float32) for w in (out_weight, other_weight)
        )

    rows = queries.shape[0]
    f32, bf16 = jnp.float32, jnp.bfloat16

    def both(parts, unit):
        return jnp.concatenate([p[unit * rows : (unit + 1) * rows] for p in parts], axis=1)

    far = products(4, 0, 1)
    far_up = shift(far[0].astype(bf16), "z", 1)
    far_down = shift(far[1].astype(bf16), "z", -1)
    middle = products(2, 1, 4)
    width = far_up.shape[1]
    zero = jnp.zeros((rows, width), f32)
    third = both(middle, 1) + jnp.concatenate([far_up.astype(f32), zero], axis=1)
    minus_third = both(middle, 2) + jnp.concatenate([zero, far_down.astype(f32)], axis=1)
    up2 = shift(jnp.concatenate([both(middle, 0), third], axis=0).astype(bf16), "z", 2)
    down2 = shift(jnp.concatenate([both(middle, 3), minus_third], axis=0).astype(bf16), "z", -2)
    near = products(7, 0, 3)
    up1 = shift((both(near, 2) + up2[rows:].astype(f32)).astype(bf16), "z", 1)
    down1 = shift((both(near, 0) + down2[rows:].astype(f32)).astype(bf16), "z", -1)
    total = (
        both(near, 1)
        + up2[:rows].astype(f32)
        + down2[:rows].astype(f32)
        + up1.astype(f32)
        + down1.astype(f32)
    ).astype(bf16)
    mine, theirs = total[:, :width], swap(total[:, width:])
    return jnp.where(
        core == 0,
        jnp.concatenate([mine, theirs], axis=0),
        jnp.concatenate([theirs, mine], axis=0),
    )


def solution(mesh):
    fine = Mesh(mesh.devices.reshape(4, 8, 2, 8), ("dp", "y", "core", "z"))
    ctx = ("y", "core")
    in_specs = (
        P(("dp", "z"), ctx),
        P(("dp", "y", "core"), "z"),
        P(ctx, "z"),
        P("z", ctx),
        P("dp"),
        P("dp"),
    )
    return jax.shard_map(
        local, mesh=fine, in_specs=in_specs, out_specs=P(("dp", "z"), ctx), check_vma=False
    )
```

```python
import functools
import math

import jax
import jax.numpy as jnp
from jax import lax
from jax.experimental import pallas as pl
from jax.experimental.pallas import tpu as pltpu
from jax.sharding import Mesh, PartitionSpec as P


HEAD = 128
RING = 8
BLOCK = 64
KEYS = 256
NEG = -1e30
EXP_SCALE = math.log2(math.e) / math.sqrt(HEAD)


def attend_kernel(base, stride, ids, lengths, order, q_ref, kv_ref, out_ref, acc_ref, top_ref):
    step = pl.program_id(0)
    unit = step // 2
    z, core = ids[0], ids[1]
    owner = (z + base + unit * stride) % RING
    first = order[(owner * 2 + core) * 2 + step % 2] * BLOCK
    heads = q_ref.shape[1] // HEAD
    rows = BLOCK * heads

    row_pos = first + lax.broadcasted_iota(jnp.int32, (BLOCK, KEYS), 0)
    row_start = jnp.zeros((BLOCK, KEYS), jnp.int32)
    lowest = jnp.int32(0)
    end = jnp.int32(0)
    for j in range(lengths.shape[0]):
        end = end + lengths[j]
        row_start = jnp.where(row_pos >= end, end, row_start)
        lowest = jnp.where(first >= end, end, lowest)
    columns = lax.broadcasted_iota(jnp.int32, (BLOCK, KEYS), 1)

    query = jnp.concatenate(
        [q_ref[:, h * HEAD : (h + 1) * HEAD] for h in range(heads)], axis=0
    )
    ones = jnp.ones((KEYS, HEAD), jnp.bfloat16)
    acc_ref[...] = jnp.zeros_like(acc_ref)
    top_ref[...] = jnp.full_like(top_ref, NEG)
    last = first // KEYS

    @pl.loop(0, last - lowest // KEYS + 1)
    def _(i):
        block = last - i
        offset = pl.multiple_of(block * KEYS, KEYS)
        keys = kv_ref[pl.ds(offset, KEYS), :HEAD]
        values = kv_ref[pl.ds(offset, KEYS), HEAD:]
        scores = lax.dot_general(
            query, keys, (((1,), (1,)), ((), ())), preferred_element_type=jnp.float32
        )
        key_pos = block * KEYS + columns
        allowed = (key_pos >= row_start) & (key_pos <= row_pos)
        scores = jnp.where(
            allowed[None], scores.reshape(heads, BLOCK, KEYS), jnp.float32(NEG)
        ).reshape(rows, KEYS)
        old = top_ref[...]
        new = jnp.maximum(old, jnp.max(scores, axis=1, keepdims=True))
        top_ref[...] = new
        keep = jnp.exp2((old - new) * EXP_SCALE)
        wide = jnp.concatenate([new, new], axis=1)
        probs = jnp.exp2((scores - wide) * EXP_SCALE).astype(jnp.bfloat16)
        both = jnp.concatenate([values, ones], axis=1)
        acc_ref[...] = acc_ref[...] * jnp.concatenate([keep, keep], axis=1) + jnp.dot(
            probs, both, preferred_element_type=jnp.float32
        )

    for h in range(heads):
        part = acc_ref[h * BLOCK : (h + 1) * BLOCK, :]
        out_ref[:, h * HEAD : (h + 1) * HEAD] = (part[:, :HEAD] / part[:, HEAD:]).astype(
            out_ref.dtype
        )


def attend(base, stride, units, ids, lengths, order, queries, kv):
    width = queries.shape[1]
    heads = width // HEAD

    def q_map(i, ids, lengths, order):
        unit = i // 2
        block = (ids[0] + base + unit * stride - ids[2] + RING) % RING
        return (block * 2 + i % 2, 0)

    return pl.pallas_call(
        functools.partial(attend_kernel, base, stride),
        out_shape=jax.ShapeDtypeStruct((units * 2 * BLOCK, width), jnp.bfloat16),
        grid_spec=pltpu.PrefetchScalarGridSpec(
            num_scalar_prefetch=3,
            grid=(units * 2,),
            in_specs=[
                pl.BlockSpec((BLOCK, width), q_map),
                pl.BlockSpec(kv.shape, lambda i, *_: (0, 0)),
            ],
            out_specs=pl.BlockSpec((BLOCK, width), lambda i, *_: (i, 0)),
            scratch_shapes=[
                pltpu.VMEM((BLOCK * heads, 2 * HEAD), jnp.float32),
                pltpu.VMEM((BLOCK * heads, HEAD), jnp.float32),
            ],
        ),
        cost_estimate=pl.CostEstimate(
            flops=units * 600_000_000, bytes_accessed=units * 1_000_000, transcendentals=units * 500_000
        ),
        name="attend",
    )(ids, lengths, order, queries, kv)


def shift(x, axis, by):
    return lax.ppermute(x, axis, [(i, (i + by) % RING) for i in range(RING)])


def swap(x):
    return lax.ppermute(x, "core", [(0, 1), (1, 0)])


def ring_gather(x, axis):
    half = x.shape[0] // 2
    ups, downs = [x], [x]
    for _ in range(3):
        ups.append(shift(ups[-1], axis, -1))
        downs.append(shift(downs[-1], axis, 1))
    top = shift(downs[3][:half], axis, 1)
    bottom = shift(ups[3][half:], axis, -1)
    return jnp.concatenate([*ups, top, bottom, *downs[:0:-1]], axis=0)


def local(tokens, queries, key_value_weight, out_weight, doc_lengths, block_order):
    z, y, core = lax.axis_index("z"), lax.axis_index("y"), lax.axis_index("core")
    ids = jnp.stack([z, core, y]).astype(jnp.int32)
    all_tokens = lax.all_gather(tokens, "z", axis=0, tiled=True)
    all_queries = ring_gather(queries, "y")
    other_weight = swap(out_weight)
    partial_kv = jnp.dot(all_tokens, key_value_weight, preferred_element_type=jnp.float32)
    partial_kv, all_queries, other_weight = lax.optimization_barrier(
        (partial_kv, all_queries, other_weight)
    )
    kv = lax.psum(partial_kv, ("y", "core")).astype(jnp.bfloat16)

    f32, bf16 = jnp.float32, jnp.bfloat16
    rows, width = queries.shape[0], out_weight.shape[1]

    def products(base, stride, units):
        attn = attend(
            base, stride, units, ids, doc_lengths, block_order, all_queries, kv
        )
        parts = [
            jnp.dot(attn, w, preferred_element_type=f32) for w in (out_weight, other_weight)
        ]
        return [
            jnp.concatenate([p[i * rows : (i + 1) * rows] for p in parts], axis=1)
            for i in range(units)
        ]

    far = products(4, 0, 1)[0].astype(bf16)
    zero = jnp.zeros((rows, width), bf16)
    up = shift(far[:, :width], "z", 1)
    down = shift(far[:, width:], "z", -1)
    up = jnp.concatenate([up, zero], axis=1)
    down = jnp.concatenate([zero, down], axis=1)
    for step in (3, 2, 1):
        ahead, behind = products(step, RING - 2 * step, 2)
        up = shift((ahead + up.astype(f32)).astype(bf16), "z", 1)
        down = shift((behind + down.astype(f32)).astype(bf16), "z", -1)
    own = products(0, 0, 1)[0]
    total = (own + up.astype(f32) + down.astype(f32)).astype(bf16)
    mine, theirs = total[:, :width], swap(total[:, width:])
    return jnp.where(
        core == 0,
        jnp.concatenate([mine, theirs], axis=0),
        jnp.concatenate([theirs, mine], axis=0),
    )


def solution(mesh):
    fine = Mesh(mesh.devices.reshape(4, 8, 2, 8), ("dp", "y", "core", "z"))
    ctx = ("y", "core")
    in_specs = (
        P(("dp", "z"), ctx),
        P(("dp", "y", "core"), "z"),
        P(ctx, "z"),
        P("z", ctx),
        P("dp"),
        P("dp"),
    )
    return jax.shard_map(
        local, mesh=fine, in_specs=in_specs, out_specs=P(("dp", "z"), ctx), check_vma=False
    )
```

```python
import functools
import math

import jax
import jax.numpy as jnp
from jax import lax
from jax.experimental import pallas as pl
from jax.experimental.pallas import tpu as pltpu
from jax.sharding import Mesh, PartitionSpec as P


HEAD = 128
RING = 8
BLOCK = 64
KEYS = 256
NEG = -1e30
EXP_SCALE = math.log2(math.e) / math.sqrt(HEAD)


def attend_kernel(base, ids, lengths, order, q_ref, kv_ref, out_ref, acc_ref):
    z, core = ids[0], ids[1]
    owner = (z + base) % RING
    first = order[(owner * 2 + core) * 2 + pl.program_id(0)] * BLOCK
    heads = q_ref.shape[1] // HEAD
    rows = BLOCK * heads

    row_pos = first + lax.broadcasted_iota(jnp.int32, (1, HEAD), 1) % BLOCK
    row_start = jnp.zeros((1, HEAD), jnp.int32)
    lowest = jnp.int32(0)
    end = jnp.int32(0)
    for j in range(lengths.shape[0]):
        end = end + lengths[j]
        row_start = jnp.where(row_pos >= end, end, row_start)
        lowest = jnp.where(first >= end, end, lowest)
    key_row = lax.broadcasted_iota(jnp.int32, (KEYS, HEAD), 0)

    query = jnp.concatenate(
        [q_ref[:, h * HEAD : (h + 1) * HEAD] for h in range(heads)], axis=0
    )
    acc_ref[...] = jnp.zeros_like(acc_ref)
    last = first // KEYS

    def visit(i, carry):
        top, total = carry
        block = last - i
        offset = pl.multiple_of(block * KEYS, KEYS)
        keys = kv_ref[pl.ds(offset, KEYS), :HEAD]
        values = kv_ref[pl.ds(offset, KEYS), HEAD:]
        scores = lax.dot_general(
            keys, query, (((1,), (1,)), ((), ())), preferred_element_type=jnp.float32
        )
        key_pos = block * KEYS + key_row
        bias = jnp.where(
            (key_pos >= row_start) & (key_pos <= row_pos), jnp.float32(0.0), jnp.float32(NEG)
        )
        scores = scores + jnp.concatenate([bias] * (rows // HEAD), axis=1)
        new = jnp.maximum(top, jnp.max(scores, axis=0, keepdims=True))
        keep = jnp.exp2((top - new) * EXP_SCALE)
        probs = jnp.exp2((scores - new) * EXP_SCALE)
        total = total * keep + jnp.sum(probs, axis=0, keepdims=True)
        acc_ref[...] = acc_ref[...] * keep + lax.dot_general(
            values,
            probs.astype(jnp.bfloat16),
            (((0,), (0,)), ((), ())),
            preferred_element_type=jnp.float32,
        )
        return new, total

    start = (jnp.full((1, rows), NEG, jnp.float32), jnp.zeros((1, rows), jnp.float32))
    _, total = lax.fori_loop(0, last - lowest // KEYS + 1, visit, start)
    scale = 1.0 / total
    for pair in range(heads // 2):
        lanes = slice(pair * HEAD, (pair + 1) * HEAD)
        turned = (acc_ref[:, lanes] * scale[:, lanes]).T.astype(out_ref.dtype)
        out_ref[:, 2 * pair * HEAD : (2 * pair + 1) * HEAD] = turned[:BLOCK]
        out_ref[:, (2 * pair + 1) * HEAD : (2 * pair + 2) * HEAD] = turned[BLOCK:]


def attend(base, ids, lengths, order, queries, kv):
    width = queries.shape[1]

    def q_map(i, ids, lengths, order):
        return ((ids[0] + base - ids[2] + RING) % RING * 2 + i, 0)

    return pl.pallas_call(
        functools.partial(attend_kernel, base),
        out_shape=jax.ShapeDtypeStruct((2 * BLOCK, width), jnp.bfloat16),
        grid_spec=pltpu.PrefetchScalarGridSpec(
            num_scalar_prefetch=3,
            grid=(2,),
            in_specs=[
                pl.BlockSpec((BLOCK, width), q_map),
                pl.BlockSpec(kv.shape, lambda i, *_: (0, 0)),
            ],
            out_specs=pl.BlockSpec((BLOCK, width), lambda i, *_: (i, 0)),
            scratch_shapes=[pltpu.VMEM((HEAD, BLOCK * (width // HEAD)), jnp.float32)],
        ),
        cost_estimate=pl.CostEstimate(
            flops=600_000_000, bytes_accessed=2_000_000, transcendentals=500_000
        ),
        name="attend",
    )(ids, lengths, order, queries, kv)


def shift(x, axis, by):
    return lax.ppermute(x, axis, [(i, (i + by) % RING) for i in range(RING)])


def swap(x):
    return lax.ppermute(x, "core", [(0, 1), (1, 0)])


def ring_gather(x, axis):
    ups, downs = [x], [x]
    for _ in range(3):
        ups.append(shift(ups[-1], axis, -1))
        downs.append(shift(downs[-1], axis, 1))
    far = shift(x, axis, RING // 2)
    return jnp.concatenate([*ups, far, *downs[:0:-1]], axis=0)


def local(tokens, queries, key_value_weight, out_weight, doc_lengths, block_order):
    z, y, core = lax.axis_index("z"), lax.axis_index("y"), lax.axis_index("core")
    ids = jnp.stack([z, core, y]).astype(jnp.int32)
    all_tokens = lax.all_gather(tokens, "z", axis=0, tiled=True)
    all_queries = ring_gather(queries, "y")
    other_weight = swap(out_weight)
    partial_kv = jnp.dot(all_tokens, key_value_weight, preferred_element_type=jnp.float32)
    partial_kv, all_queries, other_weight = lax.optimization_barrier(
        (partial_kv, all_queries, other_weight)
    )
    kv = lax.psum(partial_kv, ("y", "core")).astype(jnp.bfloat16)

    f32, bf16 = jnp.float32, jnp.bfloat16
    rows, width = queries.shape[0], out_weight.shape[1]

    def product(base):
        attn = attend(base, ids, doc_lengths, block_order, all_queries, kv)
        return jnp.concatenate(
            [jnp.dot(attn, w, preferred_element_type=f32) for w in (out_weight, other_weight)],
            axis=1,
        )

    far = product(4).astype(bf16)
    zero = jnp.zeros((rows, width), bf16)
    up = jnp.concatenate([shift(far[:, :width], "z", 1), zero], axis=1)
    down = jnp.concatenate([zero, shift(far[:, width:], "z", -1)], axis=1)
    for step in (3, 2, 1):
        up = shift((product(step) + up.astype(f32)).astype(bf16), "z", 1)
        down = shift((product(RING - step) + down.astype(f32)).astype(bf16), "z", -1)
    total = (product(0) + up.astype(f32) + down.astype(f32)).astype(bf16)
    mine, theirs = total[:, :width], swap(total[:, width:])
    return jnp.where(
        core == 0,
        jnp.concatenate([mine, theirs], axis=0),
        jnp.concatenate([theirs, mine], axis=0),
    )


def solution(mesh):
    fine = Mesh(mesh.devices.reshape(4, 8, 2, 8), ("dp", "y", "core", "z"))
    ctx = ("y", "core")
    in_specs = (
        P(("dp", "z"), ctx),
        P(("dp", "y", "core"), "z"),
        P(ctx, "z"),
        P("z", ctx),
        P("dp"),
        P("dp"),
    )
    return jax.shard_map(
        local, mesh=fine, in_specs=in_specs, out_specs=P(("dp", "z"), ctx), check_vma=False
    )
```

```python
import math

import jax
import jax.numpy as jnp
from jax import lax
from jax.experimental import pallas as pl
from jax.experimental.pallas import tpu as pltpu
from jax.sharding import Mesh, PartitionSpec as P


HEAD = 128
RING = 8
BLOCK = 64
KEYS = 256
NEG = -1e30
EXP_SCALE = math.log2(math.e) / math.sqrt(HEAD)


def attend_kernel(ids, lengths, order, q_ref, kv_ref, out_ref, acc_ref):
    z, core = ids[0], ids[1]
    step = pl.program_id(0)
    owner = (z + step // 2) % RING
    first = order[(owner * 2 + core) * 2 + step % 2] * BLOCK
    heads = q_ref.shape[1] // HEAD
    rows = BLOCK * heads

    row_pos = first + lax.broadcasted_iota(jnp.int32, (1, HEAD), 1) % BLOCK
    row_start = jnp.zeros((1, HEAD), jnp.int32)
    lowest = jnp.int32(0)
    end = jnp.int32(0)
    for j in range(lengths.shape[0]):
        end = end + lengths[j]
        row_start = jnp.where(row_pos >= end, end, row_start)
        lowest = jnp.where(first >= end, end, lowest)
    key_row = lax.broadcasted_iota(jnp.int32, (KEYS, HEAD), 0)

    query = jnp.concatenate(
        [q_ref[:, h * HEAD : (h + 1) * HEAD] for h in range(heads)], axis=0
    )
    acc_ref[...] = jnp.zeros_like(acc_ref)
    last = first // KEYS

    def visit(i, carry):
        top, total = carry
        block = last - i
        offset = pl.multiple_of(block * KEYS, KEYS)
        keys = kv_ref[pl.ds(offset, KEYS), :HEAD]
        values = kv_ref[pl.ds(offset, KEYS), HEAD:]
        scores = lax.dot_general(
            keys, query, (((1,), (1,)), ((), ())), preferred_element_type=jnp.float32
        )
        key_pos = block * KEYS + key_row
        bias = jnp.where(
            (key_pos >= row_start) & (key_pos <= row_pos), jnp.float32(0.0), jnp.float32(NEG)
        )
        scores = scores + jnp.concatenate([bias] * (rows // HEAD), axis=1)
        new = jnp.maximum(top, jnp.max(scores, axis=0, keepdims=True))
        keep = jnp.exp2((top - new) * EXP_SCALE)
        probs = jnp.exp2((scores - new) * EXP_SCALE)
        total = total * keep + jnp.sum(probs, axis=0, keepdims=True)
        acc_ref[...] = acc_ref[...] * keep + lax.dot_general(
            values,
            probs.astype(jnp.bfloat16),
            (((0,), (0,)), ((), ())),
            preferred_element_type=jnp.float32,
        )
        return new, total

    start = (jnp.full((1, rows), NEG, jnp.float32), jnp.zeros((1, rows), jnp.float32))
    _, total = lax.fori_loop(0, last - lowest // KEYS + 1, visit, start)
    scale = 1.0 / total
    for pair in range(heads // 2):
        lanes = slice(pair * HEAD, (pair + 1) * HEAD)
        turned = (acc_ref[:, lanes] * scale[:, lanes]).T.astype(out_ref.dtype)
        out_ref[:, 2 * pair * HEAD : (2 * pair + 1) * HEAD] = turned[:BLOCK]
        out_ref[:, (2 * pair + 1) * HEAD : (2 * pair + 2) * HEAD] = turned[BLOCK:]


def attend(ids, lengths, order, queries, kv):
    total, width = queries.shape

    def q_map(i, ids, lengths, order):
        return ((ids[0] + i // 2 - ids[2] + RING) % RING * 2 + i % 2, 0)

    return pl.pallas_call(
        attend_kernel,
        out_shape=jax.ShapeDtypeStruct(queries.shape, jnp.bfloat16),
        grid_spec=pltpu.PrefetchScalarGridSpec(
            num_scalar_prefetch=3,
            grid=(total // BLOCK,),
            in_specs=[
                pl.BlockSpec((BLOCK, width), q_map),
                pl.BlockSpec(kv.shape, lambda i, *_: (0, 0)),
            ],
            out_specs=pl.BlockSpec((BLOCK, width), lambda i, *_: (i, 0)),
            scratch_shapes=[pltpu.VMEM((HEAD, BLOCK * (width // HEAD)), jnp.float32)],
        ),
        cost_estimate=pl.CostEstimate(
            flops=4_800_000_000, bytes_accessed=6_000_000, transcendentals=5_000_000
        ),
        name="attend",
    )(ids, lengths, order, queries, kv)


def shift(x, axis, by):
    return lax.ppermute(x, axis, [(i, (i + by) % RING) for i in range(RING)])


def swap(x):
    return lax.ppermute(x, "core", [(0, 1), (1, 0)])


def ring_gather(x, axis):
    half = x.shape[0] // 2
    ups, downs = [x], [x]
    for _ in range(3):
        ups.append(shift(ups[-1], axis, -1))
        downs.append(shift(downs[-1], axis, 1))
    top = shift(downs[3][:half], axis, 1)
    bottom = shift(ups[3][half:], axis, -1)
    return jnp.concatenate([*ups, top, bottom, *downs[:0:-1]], axis=0)


def local(tokens, queries, key_value_weight, out_weight, doc_lengths, block_order):
    z, y, core = lax.axis_index("z"), lax.axis_index("y"), lax.axis_index("core")
    ids = jnp.stack([z, core, y]).astype(jnp.int32)
    all_tokens = lax.all_gather(tokens, "z", axis=0, tiled=True)
    all_queries = ring_gather(queries, "y")
    other_weight = swap(out_weight)
    partial_kv = jnp.dot(all_tokens, key_value_weight, preferred_element_type=jnp.float32)
    partial_kv, all_queries, other_weight = lax.optimization_barrier(
        (partial_kv, all_queries, other_weight)
    )
    kv = lax.psum(partial_kv, ("y", "core")).astype(jnp.bfloat16)

    f32, bf16 = jnp.float32, jnp.bfloat16
    rows, width = queries.shape[0], out_weight.shape[1]

    attn = attend(ids, doc_lengths, block_order, all_queries, kv)
    out = [
        jnp.dot(attn, w, preferred_element_type=f32).astype(bf16)
        for w in (out_weight, other_weight)
    ]

    def product(step):
        here = slice(step * rows, (step + 1) * rows)
        return jnp.concatenate([part[here] for part in out], axis=1).astype(f32)

    far = slice(4 * rows, 5 * rows)
    zero = jnp.zeros((rows, width), bf16)
    up = jnp.concatenate([shift(out[0][far], "z", 1), zero], axis=1)
    down = jnp.concatenate([zero, shift(out[1][far], "z", -1)], axis=1)
    for step in (3, 2, 1):
        up = shift((product(step) + up.astype(f32)).astype(bf16), "z", 1)
        down = shift((product(RING - step) + down.astype(f32)).astype(bf16), "z", -1)
    total = (product(0) + up.astype(f32) + down.astype(f32)).astype(bf16)
    mine, theirs = total[:, :width], swap(total[:, width:])
    return jnp.where(
        core == 0,
        jnp.concatenate([mine, theirs], axis=0),
        jnp.concatenate([theirs, mine], axis=0),
    )


def solution(mesh):
    fine = Mesh(mesh.devices.reshape(4, 8, 2, 8), ("dp", "y", "core", "z"))
    ctx = ("y", "core")
    in_specs = (
        P(("dp", "z"), ctx),
        P(("dp", "y", "core"), "z"),
        P(ctx, "z"),
        P("z", ctx),
        P("dp"),
        P("dp"),
    )
    return jax.shard_map(
        local, mesh=fine, in_specs=in_specs, out_specs=P(("dp", "z"), ctx), check_vma=False
    )
```

```python
import math

import jax
import jax.numpy as jnp
from jax import lax
from jax.experimental import pallas as pl
from jax.experimental.pallas import tpu as pltpu
from jax.sharding import Mesh, PartitionSpec as P


HEAD = 128
RING = 8
BLOCK = 64
KEYS = 256
NEG = -1e30
EXP_SCALE = math.log2(math.e) / math.sqrt(HEAD)


def attend_kernel(ids, lengths, order, *refs):
    *pieces, kv_ref, out_ref, acc_ref, q_ref, sems = refs
    z, core = ids[0], ids[1]
    step = pl.program_id(0)
    owner = (z + step // 2) % RING
    first = order[(owner * 2 + core) * 2 + step % 2] * BLOCK
    heads = q_ref.shape[1] // HEAD
    rows = BLOCK * heads

    @pl.when(step == 0)
    def _():
        copies, place = [], 0
        for i, piece in enumerate(pieces):
            here = q_ref.at[pl.ds(place, piece.shape[0])]
            copies.append(pltpu.make_async_copy(piece, here, sems.at[i]))
            place += piece.shape[0]
        for copy in copies:
            copy.start()
        for copy in copies:
            copy.wait()

    near = (owner - ids[2] + RING) % RING * 2 + step % 2
    here = pl.ds(pl.multiple_of(near * BLOCK, BLOCK), BLOCK)

    row_pos = first + lax.broadcasted_iota(jnp.int32, (1, HEAD), 1) % BLOCK
    row_start = jnp.zeros((1, HEAD), jnp.int32)
    lowest = jnp.int32(0)
    end = jnp.int32(0)
    for j in range(lengths.shape[0]):
        end = end + lengths[j]
        row_start = jnp.where(row_pos >= end, end, row_start)
        lowest = jnp.where(first >= end, end, lowest)
    key_row = lax.broadcasted_iota(jnp.int32, (KEYS, HEAD), 0)

    query = jnp.concatenate(
        [q_ref[here, h * HEAD : (h + 1) * HEAD] for h in range(heads)], axis=0
    )
    acc_ref[...] = jnp.zeros_like(acc_ref)
    last = first // KEYS

    def visit(i, carry):
        top, total = carry
        block = last - i
        offset = pl.multiple_of(block * KEYS, KEYS)
        keys = kv_ref[pl.ds(offset, KEYS), :HEAD]
        values = kv_ref[pl.ds(offset, KEYS), HEAD:]
        scores = lax.dot_general(
            keys, query, (((1,), (1,)), ((), ())), preferred_element_type=jnp.float32
        )
        base = block * KEYS
        bias = jnp.where(
            (key_row >= row_start - base) & (key_row <= row_pos - base),
            jnp.float32(0.0),
            jnp.float32(NEG),
        )
        scores = scores + jnp.concatenate([bias] * (rows // HEAD), axis=1)
        new = jnp.maximum(top, jnp.max(scores, axis=0, keepdims=True))
        keep = jnp.exp2((top - new) * EXP_SCALE)
        probs = jnp.exp2((scores - new) * EXP_SCALE)
        total = total * keep + jnp.sum(probs, axis=0, keepdims=True)
        acc_ref[...] = acc_ref[...] * keep + lax.dot_general(
            values,
            probs.astype(jnp.bfloat16),
            (((0,), (0,)), ((), ())),
            preferred_element_type=jnp.float32,
        )
        return new, total

    start = (jnp.full((1, rows), NEG, jnp.float32), jnp.zeros((1, rows), jnp.float32))
    _, total = lax.fori_loop(0, last - lowest // KEYS + 1, visit, start)
    scale = 1.0 / total
    for pair in range(heads // 2):
        lanes = slice(pair * HEAD, (pair + 1) * HEAD)
        turned = (acc_ref[:, lanes] * scale[:, lanes]).T.astype(out_ref.dtype)
        out_ref[:, 2 * pair * HEAD : (2 * pair + 1) * HEAD] = turned[:BLOCK]
        out_ref[:, (2 * pair + 1) * HEAD : (2 * pair + 2) * HEAD] = turned[BLOCK:]


def attend(ids, lengths, order, pieces, kv):
    width = pieces[0].shape[1]
    total = sum(piece.shape[0] for piece in pieces)
    return pl.pallas_call(
        attend_kernel,
        out_shape=jax.ShapeDtypeStruct((total, width), jnp.bfloat16),
        grid_spec=pltpu.PrefetchScalarGridSpec(
            num_scalar_prefetch=3,
            grid=(total // BLOCK,),
            in_specs=[pl.BlockSpec(memory_space=pl.ANY)] * len(pieces)
            + [pl.BlockSpec(kv.shape, lambda i, *_: (0, 0))],
            out_specs=pl.BlockSpec((BLOCK, width), lambda i, *_: (i, 0)),
            scratch_shapes=[
                pltpu.VMEM((HEAD, BLOCK * (width // HEAD)), jnp.float32),
                pltpu.VMEM((total, width), jnp.bfloat16),
                pltpu.SemaphoreType.DMA((len(pieces),)),
            ],
        ),
        cost_estimate=pl.CostEstimate(
            flops=4_800_000_000, bytes_accessed=6_000_000, transcendentals=5_000_000
        ),
        name="attend",
    )(ids, lengths, order, *pieces, kv)


def shift(x, axis, by):
    return lax.ppermute(x, axis, [(i, (i + by) % RING) for i in range(RING)])


def swap(x):
    return lax.ppermute(x, "core", [(0, 1), (1, 0)])


def ring_gather(x, axis):
    half = x.shape[0] // 2
    ups, downs = [x], [x]
    for _ in range(3):
        ups.append(shift(ups[-1], axis, -1))
        downs.append(shift(downs[-1], axis, 1))
    top = shift(downs[3][:half], axis, 1)
    bottom = shift(ups[3][half:], axis, -1)
    return [*ups, top, bottom, *downs[:0:-1]]


def local(tokens, queries, key_value_weight, out_weight, doc_lengths, block_order):
    z, y, core = lax.axis_index("z"), lax.axis_index("y"), lax.axis_index("core")
    ids = jnp.stack([z, core, y]).astype(jnp.int32)
    all_tokens = lax.all_gather(tokens, "z", axis=0, tiled=True)
    all_queries = ring_gather(queries, "y")
    other_weight = swap(out_weight)
    partial_kv = jnp.dot(all_tokens, key_value_weight, preferred_element_type=jnp.float32)
    partial_kv, other_weight = lax.optimization_barrier((partial_kv, other_weight))
    kv = lax.psum(partial_kv, ("y", "core")).astype(jnp.bfloat16)

    f32, bf16 = jnp.float32, jnp.bfloat16
    rows, width = queries.shape[0], out_weight.shape[1]

    attn = attend(ids, doc_lengths, block_order, all_queries, kv)
    far = slice(4 * rows, 5 * rows)
    first = [
        jnp.dot(attn[far], w, preferred_element_type=f32).astype(bf16)
        for w in (out_weight, other_weight)
    ]
    out = [
        jnp.dot(attn, w, preferred_element_type=f32).astype(bf16)
        for w in (out_weight, other_weight)
    ]

    def product(step):
        here = slice(step * rows, (step + 1) * rows)
        return jnp.concatenate([part[here] for part in out], axis=1).astype(f32)

    zero = jnp.zeros((rows, width), bf16)
    up = jnp.concatenate([shift(first[0], "z", 1), zero], axis=1)
    down = jnp.concatenate([zero, shift(first[1], "z", -1)], axis=1)
    for step in (3, 2, 1):
        up = shift((product(step) + up.astype(f32)).astype(bf16), "z", 1)
        down = shift((product(RING - step) + down.astype(f32)).astype(bf16), "z", -1)
    total = (product(0) + up.astype(f32) + down.astype(f32)).astype(bf16)
    mine, theirs = total[:, :width], swap(total[:, width:])
    return jnp.where(
        core == 0,
        jnp.concatenate([mine, theirs], axis=0),
        jnp.concatenate([theirs, mine], axis=0),
    )


def solution(mesh):
    fine = Mesh(mesh.devices.reshape(4, 8, 2, 8), ("dp", "y", "core", "z"))
    ctx = ("y", "core")
    in_specs = (
        P(("dp", "z"), ctx),
        P(("dp", "y", "core"), "z"),
        P(ctx, "z"),
        P("z", ctx),
        P("dp"),
        P("dp"),
    )
    return jax.shard_map(
        local, mesh=fine, in_specs=in_specs, out_specs=P(("dp", "z"), ctx), check_vma=False
    )
```

```python
import math

import jax
import jax.numpy as jnp
from jax import lax
from jax.experimental import pallas as pl
from jax.experimental.pallas import tpu as pltpu
from jax.sharding import Mesh, PartitionSpec as P


HEAD = 128
RING = 8
BLOCK = 64
KEYS = 256
NEG = -1e30
EXP_SCALE = math.log2(math.e) / math.sqrt(HEAD)


def attend_kernel(ids, lengths, order, *refs):
    *pieces, kv_ref, out_ref, acc_ref, q_ref, sems = refs
    z, core = ids[0], ids[1]
    step = pl.program_id(0)
    owner = (z + step // 2) % RING
    first = order[(owner * 2 + core) * 2 + step % 2] * BLOCK
    heads = q_ref.shape[1] // HEAD
    rows = BLOCK * heads

    @pl.when(step == 0)
    def _():
        copies, place = [], 0
        for i, piece in enumerate(pieces):
            here = q_ref.at[pl.ds(place, piece.shape[0])]
            copies.append(pltpu.make_async_copy(piece, here, sems.at[i]))
            place += piece.shape[0]
        for copy in copies:
            copy.start()
        for copy in copies:
            copy.wait()

    near = (owner - ids[2] + RING) % RING * 2 + step % 2
    here = pl.ds(pl.multiple_of(near * BLOCK, BLOCK), BLOCK)

    row_pos = first + lax.broadcasted_iota(jnp.int32, (1, HEAD), 1) % BLOCK
    row_start = jnp.zeros((1, HEAD), jnp.int32)
    lowest = jnp.int32(0)
    end = jnp.int32(0)
    for j in range(lengths.shape[0]):
        end = end + lengths[j]
        row_start = jnp.where(row_pos >= end, end, row_start)
        lowest = jnp.where(first >= end, end, lowest)
    key_row = lax.broadcasted_iota(jnp.int32, (KEYS, HEAD), 0)

    query = jnp.concatenate(
        [q_ref[here, h * HEAD : (h + 1) * HEAD] for h in range(heads)], axis=0
    )
    acc_ref[...] = jnp.zeros_like(acc_ref)
    stop = first + BLOCK

    def visit(i, carry):
        top, total = carry
        limit = stop - i * KEYS
        base = pl.multiple_of(jnp.maximum(limit - KEYS, 0), BLOCK)
        keys = kv_ref[pl.ds(base, KEYS), :HEAD]
        values = kv_ref[pl.ds(base, KEYS), HEAD:]
        scores = lax.dot_general(
            keys, query, (((1,), (1,)), ((), ())), preferred_element_type=jnp.float32
        )
        newest = jnp.minimum(row_pos, limit - 1) - base
        bias = jnp.where(
            (key_row >= row_start - base) & (key_row <= newest),
            jnp.float32(0.0),
            jnp.float32(NEG),
        )
        scores = scores + jnp.concatenate([bias] * (rows // HEAD), axis=1)
        new = jnp.maximum(top, jnp.max(scores, axis=0, keepdims=True))
        keep = jnp.exp2((top - new) * EXP_SCALE)
        probs = jnp.exp2((scores - new) * EXP_SCALE)
        total = total * keep + jnp.sum(probs, axis=0, keepdims=True)
        acc_ref[...] = acc_ref[...] * keep + lax.dot_general(
            values,
            probs.astype(jnp.bfloat16),
            (((0,), (0,)), ((), ())),
            preferred_element_type=jnp.float32,
        )
        return new, total

    start = (jnp.full((1, rows), NEG, jnp.float32), jnp.zeros((1, rows), jnp.float32))
    _, total = lax.fori_loop(0, (stop - lowest + KEYS - 1) // KEYS, visit, start)
    scale = 1.0 / total
    for pair in range(heads // 2):
        lanes = slice(pair * HEAD, (pair + 1) * HEAD)
        turned = (acc_ref[:, lanes] * scale[:, lanes]).astype(out_ref.dtype).T
        out_ref[:, 2 * pair * HEAD : (2 * pair + 1) * HEAD] = turned[:BLOCK]
        out_ref[:, (2 * pair + 1) * HEAD : (2 * pair + 2) * HEAD] = turned[BLOCK:]


def attend(ids, lengths, order, pieces, kv):
    width = pieces[0].shape[1]
    total = sum(piece.shape[0] for piece in pieces)
    return pl.pallas_call(
        attend_kernel,
        out_shape=jax.ShapeDtypeStruct((total, width), jnp.bfloat16),
        grid_spec=pltpu.PrefetchScalarGridSpec(
            num_scalar_prefetch=3,
            grid=(total // BLOCK,),
            in_specs=[pl.BlockSpec(memory_space=pl.ANY)] * len(pieces)
            + [pl.BlockSpec(kv.shape, lambda i, *_: (0, 0))],
            out_specs=pl.BlockSpec((BLOCK, width), lambda i, *_: (i, 0)),
            scratch_shapes=[
                pltpu.VMEM((HEAD, BLOCK * (width // HEAD)), jnp.float32),
                pltpu.VMEM((total, width), jnp.bfloat16),
                pltpu.SemaphoreType.DMA((len(pieces),)),
            ],
        ),
        cost_estimate=pl.CostEstimate(
            flops=4_800_000_000, bytes_accessed=6_000_000, transcendentals=5_000_000
        ),
        name="attend",
    )(ids, lengths, order, *pieces, kv)


def shift(x, axis, by):
    return lax.ppermute(x, axis, [(i, (i + by) % RING) for i in range(RING)])


def swap(x):
    return lax.ppermute(x, "core", [(0, 1), (1, 0)])


def ring_gather(x, axis):
    half = x.shape[0] // 2
    ups, downs = [x], [x]
    for _ in range(3):
        ups.append(shift(ups[-1], axis, -1))
        downs.append(shift(downs[-1], axis, 1))
    top = shift(downs[3][:half], axis, 1)
    bottom = shift(ups[3][half:], axis, -1)
    return [*ups, top, bottom, *downs[:0:-1]]


def local(tokens, queries, key_value_weight, out_weight, doc_lengths, block_order):
    z, y, core = lax.axis_index("z"), lax.axis_index("y"), lax.axis_index("core")
    ids = jnp.stack([z, core, y]).astype(jnp.int32)
    all_tokens = lax.all_gather(tokens, "z", axis=0, tiled=True)
    all_queries = ring_gather(queries, "y")
    other_weight = swap(out_weight)
    partial_kv = jnp.dot(all_tokens, key_value_weight, preferred_element_type=jnp.float32)
    partial_kv, other_weight = lax.optimization_barrier((partial_kv, other_weight))
    kv = lax.psum(partial_kv, ("y", "core")).astype(jnp.bfloat16)

    f32, bf16 = jnp.float32, jnp.bfloat16
    rows, width = queries.shape[0], out_weight.shape[1]

    attn = attend(ids, doc_lengths, block_order, all_queries, kv)
    far = slice(4 * rows, 5 * rows)
    first = [
        jnp.dot(attn[far], w, preferred_element_type=f32).astype(bf16)
        for w in (out_weight, other_weight)
    ]
    out = [
        jnp.dot(attn, w, preferred_element_type=f32).astype(bf16)
        for w in (out_weight, other_weight)
    ]

    def product(step):
        here = slice(step * rows, (step + 1) * rows)
        return jnp.concatenate([part[here] for part in out], axis=1).astype(f32)

    zero = jnp.zeros((rows, width), bf16)
    up = jnp.concatenate([shift(first[0], "z", 1), zero], axis=1)
    down = jnp.concatenate([zero, shift(first[1], "z", -1)], axis=1)
    for step in (3, 2, 1):
        up = shift((product(step) + up.astype(f32)).astype(bf16), "z", 1)
        down = shift((product(RING - step) + down.astype(f32)).astype(bf16), "z", -1)
    total = (product(0) + up.astype(f32) + down.astype(f32)).astype(bf16)
    mine, theirs = total[:, :width], swap(total[:, width:])
    return jnp.where(
        core == 0,
        jnp.concatenate([mine, theirs], axis=0),
        jnp.concatenate([theirs, mine], axis=0),
    )


def solution(mesh):
    fine = Mesh(mesh.devices.reshape(4, 8, 2, 8), ("dp", "y", "core", "z"))
    ctx = ("y", "core")
    in_specs = (
        P(("dp", "z"), ctx),
        P(("dp", "y", "core"), "z"),
        P(ctx, "z"),
        P("z", ctx),
        P("dp"),
        P("dp"),
    )
    return jax.shard_map(
        local, mesh=fine, in_specs=in_specs, out_specs=P(("dp", "z"), ctx), check_vma=False
    )
```

```python
import functools
import math

import jax
import jax.numpy as jnp
from jax import lax
from jax.experimental import pallas as pl
from jax.experimental.pallas import tpu as pltpu
from jax.sharding import Mesh, PartitionSpec as P


HEAD = 128
RING = 8
BLOCK = 64
KEYS = 256
NEG = -1e30
EXP_SCALE = math.log2(math.e) / math.sqrt(HEAD)


def attend_kernel(half, from_self, ids, lengths, order, *refs):
    *pieces, kv_ref, out_ref, acc_ref, q_ref, sems = refs
    z, core = ids[0], ids[1]
    step = pl.program_id(0)
    owner = (z + step) % RING if from_self else step
    first = order[(owner * 2 + core) * 2 + half] * BLOCK
    heads = q_ref.shape[1] // HEAD
    rows = BLOCK * heads

    @pl.when(step == 0)
    def _():
        copies = []
        for i, piece in enumerate(pieces):
            rows_here = pl.ds(half * BLOCK if piece.shape[0] > BLOCK else 0, BLOCK)
            target = q_ref.at[pl.ds(i * BLOCK, BLOCK)]
            copies.append(pltpu.make_async_copy(piece.at[rows_here], target, sems.at[i]))
        for copy in copies:
            copy.start()
        for copy in copies:
            copy.wait()

    near = (owner - ids[2] + RING) % RING
    here = pl.ds(pl.multiple_of(near * BLOCK, BLOCK), BLOCK)

    row_pos = first + lax.broadcasted_iota(jnp.int32, (1, HEAD), 1) % BLOCK
    row_start = jnp.zeros((1, HEAD), jnp.int32)
    lowest = jnp.int32(0)
    end = jnp.int32(0)
    for j in range(lengths.shape[0]):
        end = end + lengths[j]
        row_start = jnp.where(row_pos >= end, end, row_start)
        lowest = jnp.where(first >= end, end, lowest)
    key_row = lax.broadcasted_iota(jnp.int32, (KEYS, HEAD), 0)

    query = jnp.concatenate(
        [q_ref[here, h * HEAD : (h + 1) * HEAD] for h in range(heads)], axis=0
    )
    acc_ref[...] = jnp.zeros_like(acc_ref)
    stop = first + BLOCK

    def visit(i, carry):
        top, total = carry
        limit = stop - i * KEYS
        base = pl.multiple_of(jnp.maximum(limit - KEYS, 0), BLOCK)
        keys = kv_ref[pl.ds(base, KEYS), :HEAD]
        values = kv_ref[pl.ds(base, KEYS), HEAD:]
        scores = lax.dot_general(
            keys, query, (((1,), (1,)), ((), ())), preferred_element_type=jnp.float32
        )
        newest = jnp.minimum(row_pos, limit - 1) - base
        bias = jnp.where(
            (key_row >= row_start - base) & (key_row <= newest),
            jnp.float32(0.0),
            jnp.float32(NEG),
        )
        scores = scores + jnp.concatenate([bias] * (rows // HEAD), axis=1)
        new = jnp.maximum(top, jnp.max(scores, axis=0, keepdims=True))
        keep = jnp.exp2((top - new) * EXP_SCALE)
        probs = jnp.exp2((scores - new) * EXP_SCALE)
        total = total * keep + jnp.sum(probs, axis=0, keepdims=True)
        acc_ref[...] = acc_ref[...] * keep + lax.dot_general(
            values,
            probs.astype(jnp.bfloat16),
            (((0,), (0,)), ((), ())),
            preferred_element_type=jnp.float32,
        )
        return new, total

    start = (jnp.full((1, rows), NEG, jnp.float32), jnp.zeros((1, rows), jnp.float32))
    _, total = lax.fori_loop(0, (stop - lowest + KEYS - 1) // KEYS, visit, start)
    scale = 1.0 / total
    for pair in range(heads // 2):
        lanes = slice(pair * HEAD, (pair + 1) * HEAD)
        turned = (acc_ref[:, lanes] * scale[:, lanes]).astype(out_ref.dtype).T
        out_ref[:, 2 * pair * HEAD : (2 * pair + 1) * HEAD] = turned[:BLOCK]
        out_ref[:, (2 * pair + 1) * HEAD : (2 * pair + 2) * HEAD] = turned[BLOCK:]


def attend(half, from_self, ids, lengths, order, pieces, kv):
    width = pieces[0].shape[1]
    total = len(pieces) * BLOCK
    return pl.pallas_call(
        functools.partial(attend_kernel, half, from_self),
        out_shape=jax.ShapeDtypeStruct((total, width), jnp.bfloat16),
        grid_spec=pltpu.PrefetchScalarGridSpec(
            num_scalar_prefetch=3,
            grid=(total // BLOCK,),
            in_specs=[pl.BlockSpec(memory_space=pl.ANY)] * len(pieces)
            + [pl.BlockSpec(kv.shape, lambda i, *_: (0, 0))],
            out_specs=pl.BlockSpec((BLOCK, width), lambda i, *_: (i, 0)),
            scratch_shapes=[
                pltpu.VMEM((HEAD, BLOCK * (width // HEAD)), jnp.float32),
                pltpu.VMEM((total, width), jnp.bfloat16),
                pltpu.SemaphoreType.DMA((len(pieces),)),
            ],
        ),
        cost_estimate=pl.CostEstimate(
            flops=2_400_000_000, bytes_accessed=4_000_000, transcendentals=2_500_000
        ),
        name="attend",
    )(ids, lengths, order, *pieces, kv)


def shift(x, axis, by):
    return lax.ppermute(x, axis, [(i, (i + by) % RING) for i in range(RING)])


def swap(x):
    return lax.ppermute(x, "core", [(0, 1), (1, 0)])


def ring_gather(x, axis):
    half = x.shape[0] // 2
    ups, downs = [x], [x]
    for _ in range(3):
        ups.append(shift(ups[-1], axis, -1))
        downs.append(shift(downs[-1], axis, 1))
    top = shift(downs[3][:half], axis, 1)
    bottom = shift(ups[3][half:], axis, -1)
    return [[*ups, far, *downs[:0:-1]] for far in (top, bottom)]


def local(tokens, queries, key_value_weight, out_weight, doc_lengths, block_order):
    z, y, core = lax.axis_index("z"), lax.axis_index("y"), lax.axis_index("core")
    ids = jnp.stack([z, core, y]).astype(jnp.int32)
    all_tokens = lax.all_gather(tokens, "z", axis=0, tiled=True)
    all_queries = ring_gather(queries, "y")
    other_weight = swap(out_weight)
    partial_kv = jnp.dot(all_tokens, key_value_weight, preferred_element_type=jnp.float32)
    partial_kv, other_weight = lax.optimization_barrier((partial_kv, other_weight))
    kv = lax.psum(partial_kv, ("y", "core")).astype(jnp.bfloat16)

    f32, bf16 = jnp.float32, jnp.bfloat16
    rows, width = BLOCK, out_weight.shape[1]

    weights = (out_weight, other_weight)
    early = attend(0, False, ids, doc_lengths, block_order, all_queries[0], kv)
    early_out = jnp.concatenate(
        [jnp.dot(early, w, preferred_element_type=f32).astype(bf16) for w in weights], axis=1
    )
    early_sum = lax.psum_scatter(early_out, "z", scatter_dimension=0, tiled=True)
    attn = attend(1, True, ids, doc_lengths, block_order, all_queries[1], kv)
    far = slice(4 * rows, 5 * rows)
    first = [
        jnp.dot(attn[far], w, preferred_element_type=f32).astype(bf16)
        for w in weights
    ]
    out = [
        jnp.dot(attn, w, preferred_element_type=f32).astype(bf16)
        for w in weights
    ]

    def product(step):
        here = slice(step * rows, (step + 1) * rows)
        return jnp.concatenate([part[here] for part in out], axis=1).astype(f32)

    zero = jnp.zeros((rows, width), bf16)
    up = jnp.concatenate([shift(first[0], "z", 1), zero], axis=1)
    down = jnp.concatenate([zero, shift(first[1], "z", -1)], axis=1)
    for step in (3, 2, 1):
        up = shift((product(step) + up.astype(f32)).astype(bf16), "z", 1)
        down = shift((product(RING - step) + down.astype(f32)).astype(bf16), "z", -1)
    total = (product(0) + up.astype(f32) + down.astype(f32)).astype(bf16)
    total = jnp.concatenate([early_sum, total], axis=0)
    mine, theirs = total[:, :width], swap(total[:, width:])
    return jnp.where(
        core == 0,
        jnp.concatenate([mine, theirs], axis=0),
        jnp.concatenate([theirs, mine], axis=0),
    )


def solution(mesh):
    fine = Mesh(mesh.devices.reshape(4, 8, 2, 8), ("dp", "y", "core", "z"))
    ctx = ("y", "core")
    in_specs = (
        P(("dp", "z"), ctx),
        P(("dp", "y", "core"), "z"),
        P(ctx, "z"),
        P("z", ctx),
        P("dp"),
        P("dp"),
    )
    return jax.shard_map(
        local, mesh=fine, in_specs=in_specs, out_specs=P(("dp", "z"), ctx), check_vma=False
    )
```

```python
import math

import jax
import jax.numpy as jnp
from jax import lax
from jax.experimental import pallas as pl
from jax.experimental.pallas import tpu as pltpu
from jax.sharding import Mesh, PartitionSpec as P


HEAD = 128
RING = 8
BLOCK = 64
KEYS = 256
NEG = -1e30
EXP_SCALE = math.log2(math.e) / math.sqrt(HEAD)


def attend_kernel(ids, lengths, order, *refs):
    *pieces, kv, out_ref, acc_ref, q_ref, kv_ref, sems = refs
    z, core = ids[0], ids[1]
    step = pl.program_id(0)
    owner = (z + step // 2) % RING
    first = order[(owner * 2 + core) * 2 + step % 2] * BLOCK
    heads = q_ref.shape[1] // HEAD
    rows = BLOCK * heads

    @pl.when(step == 0)
    def _():
        copies, place = [pltpu.make_async_copy(kv, kv_ref, sems.at[len(pieces)])], 0
        for i, piece in enumerate(pieces):
            here = q_ref.at[pl.ds(place, piece.shape[0])]
            copies.append(pltpu.make_async_copy(piece, here, sems.at[i]))
            place += piece.shape[0]
        for copy in copies:
            copy.start()
        for copy in copies:
            copy.wait()

    near = (owner - ids[2] + RING) % RING * 2 + step % 2
    here = pl.ds(pl.multiple_of(near * BLOCK, BLOCK), BLOCK)

    row_pos = first + lax.broadcasted_iota(jnp.int32, (1, HEAD), 1) % BLOCK
    row_start = jnp.zeros((1, HEAD), jnp.int32)
    lowest = jnp.int32(0)
    end = jnp.int32(0)
    for j in range(lengths.shape[0]):
        end = end + lengths[j]
        row_start = jnp.where(row_pos >= end, end, row_start)
        lowest = jnp.where(first >= end, end, lowest)
    key_row = lax.broadcasted_iota(jnp.int32, (KEYS, HEAD), 0)

    query = jnp.concatenate(
        [q_ref[here, h * HEAD : (h + 1) * HEAD] for h in range(heads)], axis=0
    )
    acc_ref[...] = jnp.zeros_like(acc_ref)
    stop = first + BLOCK

    def visit(i, carry):
        top, total = carry
        limit = stop - i * KEYS
        base = pl.multiple_of(jnp.maximum(limit - KEYS, 0), BLOCK)
        keys = kv_ref[pl.ds(base, KEYS), :HEAD]
        values = kv_ref[pl.ds(base, KEYS), HEAD:]
        scores = lax.dot_general(
            keys, query, (((1,), (1,)), ((), ())), preferred_element_type=jnp.float32
        )
        newest = jnp.minimum(row_pos, limit - 1) - base
        bias = jnp.where(
            (key_row >= row_start - base) & (key_row <= newest),
            jnp.float32(0.0),
            jnp.float32(NEG),
        )
        scores = scores + jnp.concatenate([bias] * (rows // HEAD), axis=1)
        new = jnp.maximum(top, jnp.max(scores, axis=0, keepdims=True))
        keep = jnp.exp2((top - new) * EXP_SCALE)
        probs = jnp.exp2((scores - new) * EXP_SCALE)
        total = total * keep + jnp.sum(probs, axis=0, keepdims=True)
        acc_ref[...] = acc_ref[...] * keep + lax.dot_general(
            values,
            probs.astype(jnp.bfloat16),
            (((0,), (0,)), ((), ())),
            preferred_element_type=jnp.float32,
        )
        return new, total

    start = (jnp.full((1, rows), NEG, jnp.float32), jnp.zeros((1, rows), jnp.float32))
    _, total = lax.fori_loop(0, (stop - lowest + KEYS - 1) // KEYS, visit, start)
    scale = 1.0 / total
    for pair in range(heads // 2):
        lanes = slice(pair * HEAD, (pair + 1) * HEAD)
        turned = (acc_ref[:, lanes] * scale[:, lanes]).astype(out_ref.dtype).T
        out_ref[:, 2 * pair * HEAD : (2 * pair + 1) * HEAD] = turned[:BLOCK]
        out_ref[:, (2 * pair + 1) * HEAD : (2 * pair + 2) * HEAD] = turned[BLOCK:]


def attend(ids, lengths, order, pieces, kv):
    width = pieces[0].shape[1]
    total = sum(piece.shape[0] for piece in pieces)
    return pl.pallas_call(
        attend_kernel,
        out_shape=jax.ShapeDtypeStruct((total, width), jnp.bfloat16),
        grid_spec=pltpu.PrefetchScalarGridSpec(
            num_scalar_prefetch=3,
            grid=(total // BLOCK,),
            in_specs=[pl.BlockSpec(memory_space=pl.ANY)] * (len(pieces) + 1),
            out_specs=pl.BlockSpec((BLOCK, width), lambda i, *_: (i, 0)),
            scratch_shapes=[
                pltpu.VMEM((HEAD, BLOCK * (width // HEAD)), jnp.float32),
                pltpu.VMEM((total, width), jnp.bfloat16),
                pltpu.VMEM(kv.shape, kv.dtype),
                pltpu.SemaphoreType.DMA((len(pieces) + 1,)),
            ],
        ),
        cost_estimate=pl.CostEstimate(
            flops=4_800_000_000, bytes_accessed=6_000_000, transcendentals=5_000_000
        ),
        name="attend",
    )(ids, lengths, order, *pieces, kv)


def shift(x, axis, by):
    return lax.ppermute(x, axis, [(i, (i + by) % RING) for i in range(RING)])


def swap(x):
    return lax.ppermute(x, "core", [(0, 1), (1, 0)])


def ring_gather(x, axis):
    half = x.shape[0] // 2
    ups, downs = [x], [x]
    for _ in range(3):
        ups.append(shift(ups[-1], axis, -1))
        downs.append(shift(downs[-1], axis, 1))
    top = shift(downs[3][:half], axis, 1)
    bottom = shift(ups[3][half:], axis, -1)
    return [*ups, top, bottom, *downs[:0:-1]]


def local(tokens, queries, key_value_weight, out_weight, doc_lengths, block_order):
    z, y, core = lax.axis_index("z"), lax.axis_index("y"), lax.axis_index("core")
    ids = jnp.stack([z, core, y]).astype(jnp.int32)
    all_tokens = lax.all_gather(tokens, "z", axis=0, tiled=True)
    all_queries = ring_gather(queries, "y")
    other_weight = swap(out_weight)
    weight = jnp.concatenate([out_weight, other_weight], axis=1)
    partial_kv = jnp.dot(all_tokens, key_value_weight, preferred_element_type=jnp.float32)
    partial_kv, weight, other_weight = lax.optimization_barrier(
        (partial_kv, weight, other_weight)
    )
    kv = lax.psum(partial_kv, ("y", "core")).astype(jnp.bfloat16)

    f32, bf16 = jnp.float32, jnp.bfloat16
    rows, width = queries.shape[0], out_weight.shape[1]

    attn = attend(ids, doc_lengths, block_order, all_queries, kv)
    far = slice(4 * rows, 5 * rows)
    first = jnp.dot(attn[far], weight, preferred_element_type=f32).astype(bf16)
    out = [
        jnp.dot(attn, w, preferred_element_type=f32).astype(bf16)
        for w in (out_weight, other_weight)
    ]

    def product(step):
        here = slice(step * rows, (step + 1) * rows)
        return jnp.concatenate([part[here] for part in out], axis=1).astype(f32)

    zero = jnp.zeros((rows, width), bf16)
    up = jnp.concatenate([shift(first[:, :width], "z", 1), zero], axis=1)
    down = jnp.concatenate([zero, shift(first[:, width:], "z", -1)], axis=1)
    for step in (3, 2, 1):
        up = shift((product(step) + up.astype(f32)).astype(bf16), "z", 1)
        down = shift((product(RING - step) + down.astype(f32)).astype(bf16), "z", -1)
    total = (product(0) + up.astype(f32) + down.astype(f32)).astype(bf16)
    mine, theirs = total[:, :width], swap(total[:, width:])
    return jnp.where(
        core == 0,
        jnp.concatenate([mine, theirs], axis=0),
        jnp.concatenate([theirs, mine], axis=0),
    )


def solution(mesh):
    fine = Mesh(mesh.devices.reshape(4, 8, 2, 8), ("dp", "y", "core", "z"))
    ctx = ("y", "core")
    in_specs = (
        P(("dp", "z"), ctx),
        P(("dp", "y", "core"), "z"),
        P(ctx, "z"),
        P("z", ctx),
        P("dp"),
        P("dp"),
    )
    return jax.shard_map(
        local, mesh=fine, in_specs=in_specs, out_specs=P(("dp", "z"), ctx), check_vma=False
    )
```

```python
import math

import jax
import jax.numpy as jnp
from jax import lax
from jax.experimental import pallas as pl
from jax.experimental.pallas import tpu as pltpu
from jax.sharding import Mesh, PartitionSpec as P


HEAD = 128
RING = 8
BLOCK = 64
KEYS = 256
NEG = -1e30
EXP_SCALE = math.log2(math.e) / math.sqrt(HEAD)


def attend_kernel(ids, lengths, order, *refs):
    *pieces, kv_ref, out_ref, acc_ref, q_ref, sems = refs
    z, core = ids[0], ids[1]
    step = pl.program_id(0)
    owner = (z + step // 2) % RING
    first = order[(owner * 2 + core) * 2 + step % 2] * BLOCK
    heads = q_ref.shape[1] // HEAD
    rows = BLOCK * heads

    @pl.when(step == 0)
    def _():
        copies, place = [], 0
        for i, piece in enumerate(pieces):
            here = q_ref.at[pl.ds(place, piece.shape[0])]
            copies.append(pltpu.make_async_copy(piece, here, sems.at[i]))
            place += piece.shape[0]
        for copy in copies:
            copy.start()
        for copy in copies:
            copy.wait()

    near = (owner - ids[2] + RING) % RING * 2 + step % 2
    here = pl.ds(pl.multiple_of(near * BLOCK, BLOCK), BLOCK)

    row_pos = first + lax.broadcasted_iota(jnp.int32, (1, HEAD), 1) % BLOCK
    row_start = jnp.zeros((1, HEAD), jnp.int32)
    lowest = jnp.int32(0)
    end = jnp.int32(0)
    for j in range(lengths.shape[0]):
        end = end + lengths[j]
        row_start = jnp.where(row_pos >= end, end, row_start)
        lowest = jnp.where(first >= end, end, lowest)
    key_row = lax.broadcasted_iota(jnp.int32, (KEYS, HEAD), 0)

    query = jnp.concatenate(
        [q_ref[here, h * HEAD : (h + 1) * HEAD] for h in range(heads)], axis=0
    )
    acc_ref[...] = jnp.zeros_like(acc_ref)
    stop = first + BLOCK

    def visit(i, carry):
        top, total = carry
        limit = stop - i * KEYS
        base = pl.multiple_of(jnp.maximum(limit - KEYS, 0), BLOCK)
        keys = kv_ref[pl.ds(base, KEYS), :HEAD]
        values = kv_ref[pl.ds(base, KEYS), HEAD:]
        scores = lax.dot_general(
            keys, query, (((1,), (1,)), ((), ())), preferred_element_type=jnp.float32
        )
        newest = jnp.minimum(row_pos, limit - 1) - base
        bias = jnp.where(
            (key_row >= row_start - base) & (key_row <= newest),
            jnp.float32(0.0),
            jnp.float32(NEG),
        )
        scores = scores + jnp.concatenate([bias] * (rows // HEAD), axis=1)
        new = jnp.maximum(top, jnp.max(scores, axis=0, keepdims=True))
        keep = jnp.exp2((top - new) * EXP_SCALE)
        probs = jnp.exp2((scores - new) * EXP_SCALE)
        total = total * keep + jnp.sum(probs, axis=0, keepdims=True)
        acc_ref[...] = acc_ref[...] * keep + lax.dot_general(
            values,
            probs.astype(jnp.bfloat16),
            (((0,), (0,)), ((), ())),
            preferred_element_type=jnp.float32,
        )
        return new, total

    start = (jnp.full((1, rows), NEG, jnp.float32), jnp.zeros((1, rows), jnp.float32))
    _, total = lax.fori_loop(0, (stop - lowest + KEYS - 1) // KEYS, visit, start)
    scale = 1.0 / total
    for pair in range(heads // 2):
        lanes = slice(pair * HEAD, (pair + 1) * HEAD)
        turned = (acc_ref[:, lanes] * scale[:, lanes]).astype(out_ref.dtype).T
        out_ref[:, 2 * pair * HEAD : (2 * pair + 1) * HEAD] = turned[:BLOCK]
        out_ref[:, (2 * pair + 1) * HEAD : (2 * pair + 2) * HEAD] = turned[BLOCK:]


def attend(ids, lengths, order, pieces, kv):
    width = pieces[0].shape[1]
    total = sum(piece.shape[0] for piece in pieces)
    return pl.pallas_call(
        attend_kernel,
        out_shape=jax.ShapeDtypeStruct((total, width), jnp.bfloat16),
        grid_spec=pltpu.PrefetchScalarGridSpec(
            num_scalar_prefetch=3,
            grid=(total // BLOCK,),
            in_specs=[pl.BlockSpec(memory_space=pl.ANY)] * len(pieces)
            + [pl.BlockSpec(kv.shape, lambda i, *_: (0, 0))],
            out_specs=pl.BlockSpec((BLOCK, width), lambda i, *_: (i, 0)),
            scratch_shapes=[
                pltpu.VMEM((HEAD, BLOCK * (width // HEAD)), jnp.float32),
                pltpu.VMEM((total, width), jnp.bfloat16),
                pltpu.SemaphoreType.DMA((len(pieces),)),
            ],
        ),
        cost_estimate=pl.CostEstimate(
            flops=4_800_000_000, bytes_accessed=6_000_000, transcendentals=5_000_000
        ),
        name="attend",
    )(ids, lengths, order, *pieces, kv)


def shift(x, axis, by):
    return lax.ppermute(x, axis, [(i, (i + by) % RING) for i in range(RING)])


def swap(x):
    return lax.ppermute(x, "core", [(0, 1), (1, 0)])


def ring_gather(x, axis):
    half = x.shape[0] // 2
    ups, downs = [x], [x]
    for _ in range(3):
        ups.append(shift(ups[-1], axis, -1))
        downs.append(shift(downs[-1], axis, 1))
    top = shift(downs[3][:half], axis, 1)
    bottom = shift(ups[3][half:], axis, -1)
    return [*ups, top, bottom, *downs[:0:-1]]


def local(tokens, queries, key_value_weight, out_weight, doc_lengths, block_order):
    z, y, core = lax.axis_index("z"), lax.axis_index("y"), lax.axis_index("core")
    ids = jnp.stack([z, core, y]).astype(jnp.int32)
    all_tokens = lax.all_gather(tokens, "z", axis=0, tiled=True)
    all_queries = ring_gather(queries, "y")
    other_weight = swap(out_weight)
    partial_kv = jnp.dot(all_tokens, key_value_weight, preferred_element_type=jnp.float32)
    partial_kv, other_weight = lax.optimization_barrier((partial_kv, other_weight))
    kv = lax.psum(partial_kv, ("y", "core")).astype(jnp.bfloat16)

    f32, bf16 = jnp.float32, jnp.bfloat16
    rows, width = queries.shape[0], out_weight.shape[1]

    attn = attend(ids, doc_lengths, block_order, all_queries, kv)
    far = slice(4 * rows, 5 * rows)
    first = [
        jnp.dot(attn[far], w, preferred_element_type=f32).astype(bf16)
        for w in (out_weight, other_weight)
    ]
    out = [
        jnp.dot(attn, w, preferred_element_type=f32).astype(bf16)
        for w in (out_weight, other_weight)
    ]

    def product(step):
        here = slice(step * rows, (step + 1) * rows)
        return jnp.concatenate([part[here] for part in out], axis=1).astype(f32)

    zero = jnp.zeros((rows, width), bf16)
    up = jnp.concatenate([shift(first[0], "z", 1), zero], axis=1)
    down = jnp.concatenate([zero, shift(first[1], "z", -1)], axis=1)
    for step in (3, 2, 1):
        up = shift((product(step) + up.astype(f32)).astype(bf16), "z", 1)
        down = shift((product(RING - step) + down.astype(f32)).astype(bf16), "z", -1)
    total = (product(0) + up.astype(f32) + down.astype(f32)).astype(bf16)
    mine, theirs = total[:, :width], swap(total[:, width:])
    around = jnp.concatenate([mine, theirs, mine], axis=0)
    return lax.dynamic_slice_in_dim(around, core * mine.shape[0], 2 * mine.shape[0], 0)


def solution(mesh):
    fine = Mesh(mesh.devices.reshape(4, 8, 2, 8), ("dp", "y", "core", "z"))
    ctx = ("y", "core")
    in_specs = (
        P(("dp", "z"), ctx),
        P(("dp", "y", "core"), "z"),
        P(ctx, "z"),
        P("z", ctx),
        P("dp"),
        P("dp"),
    )
    return jax.shard_map(
        local, mesh=fine, in_specs=in_specs, out_specs=P(("dp", "z"), ctx), check_vma=False
    )
```
